32 devices in a mesh: dp: 4 (over z), expert: 4 (over y, x), tensor: 2 (over core).
Axes of the slice: x: 2, y: 2, z: 4, core: 2. Of those that a mesh axis runs over, the one named last changes fastest.
Arguments:
- tokens: bfloat16 [8192, 1536], P(('dp', 'tensor')), may hold values from -6 to 6
- deal: int32 [16], P(('dp', 'tensor')), may hold values from 0 to 15, as said below
- lengths: int32 [16], P(('dp', 'tensor')), may hold values from 256 to 512, as said below
- priority: int32 [8192], P(('dp', 'tensor')), may hold values from 0 to 511, as said below
- routes: int32 [8192, 2], P(('dp', 'tensor')), may hold values from 0 to 15, all different within a row
- gain_attn: bfloat16 [1536], P(('dp', 'tensor')), may hold values from 0.5 to 1.5
- w_query: bfloat16 [1536, 1536], P(('dp', 'tensor'), 'expert'), may hold values from -0.15625 to 0.15625
- w_key: bfloat16 [1536, 512], P(('dp', 'tensor'), 'expert'), may hold values from -0.15625 to 0.15625
- w_value: bfloat16 [1536, 512], P(('dp', 'tensor'), 'expert'), may hold values from -0.15625 to 0.15625
- w_out: bfloat16 [1536, 1536], P('expert', ('dp', 'tensor')), may hold values from -0.625 to 0.625
- gain_ffn: bfloat16 [1536], P(('dp', 'tensor')), may hold values from 0.5 to 1.5
- w_router: bfloat16 [1536, 16], P(('dp', 'tensor')), may hold values from -0.15625 to 0.15625
- w_gate: bfloat16 [16, 1536, 1024], P('expert', 'dp', 'tensor'), may hold values from -0.15625 to 0.15625
- w_up: bfloat16 [16, 1536, 1024], P('expert', 'dp', 'tensor'), may hold values from -0.15625 to 0.15625
- w_down: bfloat16 [16, 1024, 1536], P('expert', 'tensor', 'dp'), may hold values from -1.5 to 1.5
- cotangent: bfloat16 [8192, 1536], P(('dp', 'tensor')), may hold values from -6 to 6
Outputs:
- output: bfloat16 [8192, 1536], P(('dp', 'tensor'))
- d_tokens: bfloat16 [8192, 1536], P(('dp', 'tensor'))
- d_gain_attn: float32 [1536], P(('dp', 'tensor'))
- d_w_query: float32 [1536, 1536], P(('dp', 'tensor'), 'expert')
- d_w_key: float32 [1536, 512], P(('dp', 'tensor'), 'expert')
- d_w_value: float32 [1536, 512], P(('dp', 'tensor'), 'expert')
- d_w_out: float32 [1536, 1536], P('expert', ('dp', 'tensor'))
- d_gain_ffn: float32 [1536], P(('dp', 'tensor'))
- d_w_router: float32 [1536, 16], P(('dp', 'tensor'))
- d_w_gate: float32 [16, 1536, 1024], P('expert', 'dp', 'tensor')
- d_w_up: float32 [16, 1536, 1024], P('expert', 'dp', 'tensor')
- d_w_down: float32 [16, 1024, 1536], P('expert', 'tensor', 'dp')
The draws below stay inside these ranges and needn't reach their ends.
Inputs may be any that keep to these rules, and one draw needn't show every extreme that they name: A permutation of the places; for each micro-batch m there is one number k_m, 1 to 7, such that deal[o * 2 + m] = (o xor k_m) * 2 + m for every o. Each sequence's live tokens are its first lengths slots; in every draw some sequence has all 512 slots live. `priority`: within each place's 512 rows, a permutation of 0 to 511.
All inputs are finite; a program needn't handle non-finite values.
Results may differ from the reference program's by a relative error of at most 0.03.
Values may be sent and summed in bfloat16 or wider, within the bound.
No kernel may reach another device: no remote copies, remote signals or barrier semaphores. Data moves between devices by JAX's collectives and lax.ppermute only.
A program may use at most 256 MiB of HBM per device.

```python
import math
import jax
import jax.numpy as jnp
from jax import lax

D = 1536
HEADS = 24
KV_HEADS = 8
HEAD_DIM = 64
EXPERTS = 16
FF = 1024
TOP = 2
SEQ_LEN = 512
MICRO = 2
CAP = 80
SEQS = 16
TOKENS = 8192
N_EXPERT = 4


def draw_deal(key, part):
    owners = SEQS // MICRO
    masks = jax.random.randint(key, (MICRO,), 1, owners, dtype=jnp.int32)
    owner_ids = jnp.arange(owners, dtype=jnp.int32)
    micro_ids = jnp.arange(MICRO, dtype=jnp.int32)
    target = jnp.bitwise_xor(owner_ids[:, None], masks[None, :]) * MICRO + micro_ids[None, :]
    return target.reshape(SEQS).astype(jnp.int32)


def draw_lengths(key, part):
    drawn = jax.random.randint(key, (SEQS,), SEQ_LEN // 2, SEQ_LEN + 1, dtype=jnp.int32)
    chosen = jax.random.randint(jax.random.fold_in(key, 7), (), 0, SEQS, dtype=jnp.int32)
    return jnp.where(jnp.arange(SEQS, dtype=jnp.int32) == chosen, SEQ_LEN, drawn).astype(jnp.int32)


def draw_priority(key, part):
    subkeys = jax.random.split(key, SEQS)
    shuffled = jax.vmap(lambda sub_key: jax.random.permutation(sub_key, SEQ_LEN))(subkeys)
    return shuffled.reshape(TOKENS).astype(jnp.int32)


def steps_of(own_key, extent, pieces, smallest, top_value):
    gain, own = 1.0, jax.random.fold_in(own_key, 6)
    for axis_at, shards_of in pieces:
        draws = jnp.exp(jax.random.uniform(jax.random.fold_in(own, axis_at), (shards_of,), jnp.float32, smallest / len(pieces), top_value / len(pieces)))
        gain = gain * jnp.repeat(draws, extent[axis_at] // shards_of).reshape([-1 if axis == axis_at else 1 for axis in range(len(extent))])
    return gain


def different_ones(stream_key, rows, amount, top, lift):
    order = jax.random.permutation(jax.random.fold_in(stream_key, 1), amount)
    boost = order
    for power in range(3):
        boost = boost * boost // amount
    boost = boost * lift // amount
    lots = jax.random.randint(jax.random.fold_in(stream_key, 2), (rows, amount), 0, 4096) + boost
    sure = jax.random.permutation(jax.random.fold_in(stream_key, 3), rows)[jnp.arange(amount) % rows]
    lots = jnp.where(jnp.arange(rows)[:, None] == sure[None, :], 1 << 14, lots)
    score = lots * amount + jnp.arange(amount)
    return lax.top_k(score.astype(jnp.int32), top)[1].astype(jnp.int32)


def bell_draw(stream_key, dims, deviation, reach, pieces=(), held_as=jnp.bfloat16):
    level = steps_of(stream_key, dims, pieces, -0.22, 0.18) if pieces else 1.0
    values = jax.random.normal(stream_key, dims, jnp.float32) * deviation * level
    return jnp.minimum(jnp.maximum(values, -reach), reach).astype(held_as)


def setup_inputs(seed: int = 0) -> dict:
    splits = jax.random.split(jax.random.key(seed), 17)
    tokens = bell_draw(splits[0], (TOKENS, D), 1.0, 6.0, ((0, 8),))
    deal = draw_deal(jax.random.fold_in(splits[16], 71), 0)
    lengths = draw_lengths(jax.random.fold_in(splits[16], 71), 0)
    priority = draw_priority(jax.random.fold_in(splits[16], 71), 0)
    routes = different_ones(splits[4], TOKENS, EXPERTS, TOP, 1024)
    gain_attn = jnp.clip(1.0 + 0.1 * jax.random.normal(splits[5], (D,), jnp.float32), 0.5, 1.5).astype(jnp.bfloat16)
    w_query = bell_draw(splits[6], (D, HEADS * HEAD_DIM), D ** -0.5, 0.15625, ((0, 8), (1, 4)))
    w_key = bell_draw(splits[7], (D, KV_HEADS * HEAD_DIM), D ** -0.5, 0.15625, ((0, 8), (1, 4)))
    w_value = bell_draw(splits[8], (D, KV_HEADS * HEAD_DIM), D ** -0.5, 0.15625, ((0, 8), (1, 4)))
    w_out = bell_draw(splits[9], (HEADS * HEAD_DIM, D), (HEADS * HEAD_DIM // 16) ** -0.5, 0.625, ((0, 4), (1, 8)))
    gain_ffn = jnp.clip(1.0 + 0.1 * jax.random.normal(splits[10], (D,), jnp.float32), 0.5, 1.5).astype(jnp.bfloat16)
    w_router = bell_draw(splits[11], (D, EXPERTS), D ** -0.5, 0.15625, ((0, 8),))
    w_gate = bell_draw(splits[12], (EXPERTS, D, FF), D ** -0.5, 0.15625, ((0, 4), (1, 4), (2, 2)))
    w_up = bell_draw(splits[13], (EXPERTS, D, FF), D ** -0.5, 0.15625, ((0, 4), (1, 4), (2, 2)))
    w_down = bell_draw(splits[14], (EXPERTS, FF, D), (FF // 64) ** -0.5, 1.5, ((0, 4), (1, 2), (2, 4)))
    cotangent = bell_draw(splits[15], (TOKENS, D), 1.0, 6.0, ((0, 8),))
    return {"tokens": tokens, "deal": deal, "lengths": lengths, "priority": priority, "routes": routes, "gain_attn": gain_attn, "w_query": w_query, "w_key": w_key, "w_value": w_value, "w_out": w_out, "gain_ffn": gain_ffn, "w_router": w_router, "w_gate": w_gate, "w_up": w_up, "w_down": w_down, "cotangent": cotangent}


norm_epsilon = 1e-05
masked_score = -1e+30

@jax.custom_vjp
def low(v):
    return lax.optimization_barrier(v.astype(jnp.bfloat16)).astype(jnp.float32)

@jax.custom_vjp
def low_back(v):
    return v

def low_keep(v):
    return (low(v), None)

def low_pass(kept, grad):
    return (grad,)

def back_keep(v):
    return (v, None)

def back_low(kept, grad):
    return (low(grad),)
low.defvjp(low_keep, low_pass)
low_back.defvjp(back_keep, back_low)

def slotting(length_one, priority_one, route_rows):
    count = priority_one.shape[0]
    positions = jnp.arange(count, dtype=jnp.int32)
    live_rows = positions < length_one
    inverse = jnp.zeros((count,), jnp.int32).at[priority_one].set(positions)
    ranked = route_rows[inverse].reshape(-1)
    ranked_live = jnp.repeat(live_rows[inverse], TOP)
    table = ((ranked[:, None] == jnp.arange(EXPERTS, dtype=jnp.int32)[None, :]) & ranked_live[:, None]).astype(jnp.int32)
    before = jnp.cumsum(table, axis=0) - table
    place_ranked = lax.optimization_barrier(jnp.sum(before * table, axis=1)).astype(jnp.int32)
    place = place_ranked.reshape(count, TOP)[priority_one]
    kept_pair = live_rows[:, None] & (place < CAP)
    slot_index = jnp.where(kept_pair, route_rows * CAP + place, EXPERTS * CAP).astype(jnp.int32)
    pair_ids = jnp.arange(count * TOP, dtype=jnp.int32)
    slot_pair = jnp.full((EXPERTS * CAP + 1,), count * TOP, jnp.int32).at[slot_index.reshape(-1)].set(pair_ids)
    return (slot_index, slot_pair[:EXPERTS * CAP])

def layer(params_in, rows_in, length_one, slot_index, slot_pair, route_rows):
    gain_one, wquery, wkey, wvalue, wout, gain_two, wrouter, wgate, wup, wdown = params_in
    precise = lax.Precision.HIGHEST
    count = rows_in.shape[0]
    groups_per = HEADS // KV_HEADS
    scale_value = 1.0 / math.sqrt(HEAD_DIM)
    scale_one = lax.rsqrt(lax.optimization_barrier(jnp.mean(rows_in * rows_in, axis=-1, keepdims=True)) + norm_epsilon)
    normed_one = low(rows_in * scale_one * gain_one)
    query = low(low_back(jnp.dot(normed_one, wquery, precision=precise))).reshape(count, HEADS, HEAD_DIM)
    key_rows = low(low_back(jnp.dot(normed_one, wkey, precision=precise))).reshape(count, KV_HEADS, HEAD_DIM)
    value_rows = low(low_back(jnp.dot(normed_one, wvalue, precision=precise))).reshape(count, KV_HEADS, HEAD_DIM)
    key_all = jnp.repeat(key_rows, groups_per, axis=1)
    value_all = jnp.repeat(value_rows, groups_per, axis=1)
    raw_scores = jnp.einsum('qhd,khd->hqk', query, key_all, precision=precise)
    scores = low_back(raw_scores * scale_value)
    positions = jnp.arange(count, dtype=jnp.int32)
    allowed = (positions[None, :] <= positions[:, None]) & (positions[None, :] < length_one)
    probs = jax.nn.softmax(jnp.where(allowed[None], scores, masked_score), axis=-1)
    mixed = low(low_back(jnp.einsum('hqk,khd->qhd', low(probs), value_all, precision=precise)))
    mixed = mixed.reshape(count, N_EXPERT, HEADS * HEAD_DIM // N_EXPERT)
    attn_part = low(low_back(jnp.einsum('sei,eid->esd', mixed, wout.reshape(N_EXPERT, -1, D), precision=precise)))
    hidden_one = rows_in + lax.optimization_barrier(jnp.sum(attn_part, axis=0))
    scale_two = lax.rsqrt(lax.optimization_barrier(jnp.mean(hidden_one * hidden_one, axis=-1, keepdims=True)) + norm_epsilon)
    normed_two = low(hidden_one * scale_two * gain_two)
    logits = low_back(jnp.dot(normed_two, wrouter, precision=precise))
    router = jax.nn.softmax(logits, axis=-1)
    gate_values = jnp.take_along_axis(router, route_rows, axis=1)
    padded_two = jnp.concatenate([normed_two, jnp.zeros((1, D), jnp.float32)], axis=0)
    slot_rows = padded_two[slot_pair // TOP].reshape(EXPERTS, CAP, D)
    gate_in = low_back(jnp.einsum('ecd,edf->ecf', slot_rows, wgate, precision=precise))
    up_in = low_back(jnp.einsum('ecd,edf->ecf', slot_rows, wup, precision=precise))
    hidden = low(jax.nn.silu(gate_in) * up_in)
    expert_out = low_back(jnp.einsum('ecf,efd->ecd', hidden, wdown, precision=precise))
    flat_out = jnp.concatenate([expert_out.reshape(EXPERTS * CAP, D), jnp.zeros((1, D), jnp.float32)], axis=0)
    picked = flat_out[slot_index] * gate_values[:, :, None]
    owner_group = route_rows // (EXPERTS // N_EXPERT)
    select = (owner_group[None, :, :] == jnp.arange(N_EXPERT, dtype=jnp.int32)[:, None, None]).astype(jnp.float32)
    moe_part = low(jnp.einsum('esc,scd->esd', select, picked, precision=precise))
    return hidden_one + lax.optimization_barrier(jnp.sum(moe_part, axis=0))

def reference(tokens, deal, lengths, priority, routes, gain_attn, w_query, w_key, w_value, w_out, gain_ffn, w_router, w_gate, w_up, w_down, cotangent):
    params_all = tuple((array_in.astype(jnp.float32) for array_in in (gain_attn, w_query, w_key, w_value, w_out, gain_ffn, w_router, w_gate, w_up, w_down)))
    count = lengths.shape[0]
    rows_all = tokens.astype(jnp.float32).reshape(count, SEQ_LEN, D)
    grads_all = cotangent.astype(jnp.float32).reshape(count, SEQ_LEN, D)
    lengths_given = lengths[deal]
    ranks_all = priority.reshape(count, SEQ_LEN)[deal]
    routes_all = routes.reshape(count, SEQ_LEN, TOP)[deal]

    def one_sequence(running, item_in):
        rows_in, grad_rows, length_one, priority_one, route_rows = item_in
        slot_index, slot_pair = slotting(length_one, priority_one, route_rows)

        def apply_layer(params_in, layer_rows):
            return layer(params_in, layer_rows, length_one, slot_index, slot_pair, route_rows)
        result, pull_back = jax.vjp(apply_layer, params_all, rows_in)
        param_grads, row_grads = pull_back(grad_rows)
        running = jax.tree.map(lambda left, right: left + right, running, param_grads)
        return (running, (result.astype(jnp.bfloat16), row_grads.astype(jnp.bfloat16)))
    start_sums = jax.tree.map(jnp.zeros_like, params_all)
    sums_all, (results, row_grads) = lax.scan(one_sequence, start_sums, (rows_all, grads_all, lengths_given, ranks_all, routes_all))
    return (results.reshape(-1, D), row_grads.reshape(-1, D), sums_all[0], sums_all[1], sums_all[2], sums_all[3], sums_all[4], sums_all[5], sums_all[6], sums_all[7], sums_all[8], sums_all[9])
```

```python
import math

import jax
import jax.numpy as jnp
from jax import lax
from jax.experimental import pallas as pl
from jax.experimental.pallas import tpu as pltpu
from jax.sharding import PartitionSpec as P

D = 1536
HEADS = 24
KV_HEADS = 8
HEAD_DIM = 64
EXPERTS = 16
FF = 1024
TOP = 2
SEQ_LEN = 512
MICRO = 2
CAP = 80

BF = jnp.bfloat16
F32 = jnp.float32
norm_epsilon = 1e-05
masked_score = -1e30
score_scale = 1.0 / math.sqrt(HEAD_DIM)
HALF = SEQ_LEN // 2


def matmul(left, right):
    return lax.dot_general(left, right, (((1,), (0,)), ((), ())), preferred_element_type=F32)


def matmul_nt(left, right):
    return lax.dot_general(left, right, (((1,), (1,)), ((), ())), preferred_element_type=F32)


def matmul_tn(left, right):
    return lax.dot_general(left, right, (((0,), (0,)), ((), ())), preferred_element_type=F32)


def rms_scale(values):
    return lax.rsqrt(jnp.mean(values * values, axis=-1, keepdims=True) + norm_epsilon)


def swap(block, axis, distance):
    count = lax.axis_size(axis)
    return lax.ppermute(block, axis, [(low, low ^ distance) for low in range(count)])


def pick(stacked, index):
    return lax.dynamic_index_in_dim(stacked, index, 0, keepdims=False)


def attention_forward_kernel(length_ref, qkv_ref, mixed_ref, probs_low_ref, probs_high_ref):
    heads = probs_low_ref.shape[0]
    kv_heads = heads * KV_HEADS // HEADS
    groups = heads // kv_heads
    length_one = length_ref[0]
    key_base = heads * HEAD_DIM
    value_base = key_base + kv_heads * HEAD_DIM
    value_t = qkv_ref[:, value_base : value_base + kv_heads * HEAD_DIM].astype(F32).T.astype(BF)
    key_at = lax.broadcasted_iota(jnp.int32, (HALF, HALF), 0)
    query_at = lax.broadcasted_iota(jnp.int32, (HALF, HALF), 1)
    causal = key_at <= query_at
    ragged = causal & (key_at + HALF < length_one)
    for kv in range(kv_heads):
        keys = qkv_ref[:, key_base + kv * HEAD_DIM : key_base + (kv + 1) * HEAD_DIM]
        values = value_t[kv * HEAD_DIM : (kv + 1) * HEAD_DIM, :]
        for group in range(groups):
            head = kv * groups + group
            lanes = slice(head * HEAD_DIM, (head + 1) * HEAD_DIM)
            query = qkv_ref[:, lanes] * jnp.asarray(score_scale, BF)
            first = jnp.where(causal, matmul_nt(keys[:HALF], query[:HALF]), masked_score)
            first = jnp.exp(first - jnp.max(first, axis=0, keepdims=True))
            first = (first * (1.0 / jnp.sum(first, axis=0, keepdims=True))).astype(BF)
            probs_low_ref[head] = first
            upper = matmul_nt(keys[:HALF], query[HALF:])
            lower = jnp.where(ragged, matmul_nt(keys[HALF:], query[HALF:]), masked_score)
            highest = jnp.maximum(
                jnp.max(upper, axis=0, keepdims=True), jnp.max(lower, axis=0, keepdims=True)
            )
            upper = jnp.exp(upper - highest)
            lower = jnp.exp(lower - highest)
            inverse = 1.0 / (
                jnp.sum(upper, axis=0, keepdims=True) + jnp.sum(lower, axis=0, keepdims=True)
            )
            upper = (upper * inverse).astype(BF)
            lower = (lower * inverse).astype(BF)
            probs_high_ref[head, :HALF] = upper
            probs_high_ref[head, HALF:] = lower
            left = matmul(values[:, :HALF], first)
            right = matmul(values[:, :HALF], upper) + matmul(values[:, HALF:], lower)
            mixed_ref[:HALF, lanes] = left.T.astype(BF)
            mixed_ref[HALF:, lanes] = right.T.astype(BF)


def attention_forward(length_one, qkv):
    heads = qkv.shape[1] * HEADS // ((HEADS + 2 * KV_HEADS) * HEAD_DIM)
    vmem = pl.BlockSpec(memory_space=pltpu.VMEM)
    return pl.pallas_call(
        attention_forward_kernel,
        in_specs=[pl.BlockSpec(memory_space=pltpu.SMEM), vmem],
        out_specs=[vmem, vmem, vmem],
        out_shape=[
            jax.ShapeDtypeStruct((SEQ_LEN, heads * HEAD_DIM), BF),
            jax.ShapeDtypeStruct((heads, HALF, HALF), BF),
            jax.ShapeDtypeStruct((heads, SEQ_LEN, HALF), BF),
        ],
        compiler_params=pltpu.CompilerParams(vmem_limit_bytes=32 << 20),
        name="attention_forward",
    )(length_one.reshape(1), qkv)


def attention_backward_kernel(
    qkv_ref, mixed_ref, grad_ref, probs_low_ref, probs_high_ref, grad_qkv_ref
):
    heads = probs_low_ref.shape[0]
    kv_heads = heads * KV_HEADS // HEADS
    groups = heads // kv_heads
    key_base = heads * HEAD_DIM
    value_base = key_base + kv_heads * HEAD_DIM
    product_t = (mixed_ref[...].astype(F32) * grad_ref[...].astype(F32)).T
    key_t = qkv_ref[:, key_base : key_base + kv_heads * HEAD_DIM].astype(F32).T.astype(BF)
    for kv in range(kv_heads):
        keys = slice(key_base + kv * HEAD_DIM, key_base + (kv + 1) * HEAD_DIM)
        values = slice(value_base + kv * HEAD_DIM, value_base + (kv + 1) * HEAD_DIM)
        value_rows = qkv_ref[:, values]
        keys_t = key_t[kv * HEAD_DIM : (kv + 1) * HEAD_DIM, :]
        grad_key_top = grad_key_bottom = grad_value_top = grad_value_bottom = 0.0
        for group in range(groups):
            head = kv * groups + group
            lanes = slice(head * HEAD_DIM, (head + 1) * HEAD_DIM)
            inner = jnp.sum(product_t[lanes, :], axis=0, keepdims=True)
            query = qkv_ref[:, lanes] * jnp.asarray(score_scale, BF)
            grad = grad_ref[:, lanes]
            first = probs_low_ref[head]
            upper = probs_high_ref[head, :HALF]
            lower = probs_high_ref[head, HALF:]
            grad_first = matmul_nt(value_rows[:HALF], grad[:HALF]) - inner[:, :HALF]
            grad_upper = matmul_nt(value_rows[:HALF], grad[HALF:]) - inner[:, HALF:]
            grad_lower = matmul_nt(value_rows[HALF:], grad[HALF:]) - inner[:, HALF:]
            grad_first = (first.astype(F32) * grad_first).astype(BF)
            grad_upper = (upper.astype(F32) * grad_upper).astype(BF)
            grad_lower = (lower.astype(F32) * grad_lower).astype(BF)
            left = matmul(keys_t[:, :HALF], grad_first)
            right = matmul(keys_t[:, :HALF], grad_upper) + matmul(keys_t[:, HALF:], grad_lower)
            grad_qkv_ref[:HALF, lanes] = (left * score_scale).T.astype(BF)
            grad_qkv_ref[HALF:, lanes] = (right * score_scale).T.astype(BF)
            grad_key_top += matmul(grad_first, query[:HALF]) + matmul(grad_upper, query[HALF:])
            grad_key_bottom += matmul(grad_lower, query[HALF:])
            grad_value_top += matmul(first, grad[:HALF]) + matmul(upper, grad[HALF:])
            grad_value_bottom += matmul(lower, grad[HALF:])
        grad_qkv_ref[:HALF, keys] = grad_key_top.astype(BF)
        grad_qkv_ref[HALF:, keys] = grad_key_bottom.astype(BF)
        grad_qkv_ref[:HALF, values] = grad_value_top.astype(BF)
        grad_qkv_ref[HALF:, values] = grad_value_bottom.astype(BF)


def attention_backward(qkv, mixed, grad_mixed, probs_low, probs_high):
    vmem = pl.BlockSpec(memory_space=pltpu.VMEM)
    return pl.pallas_call(
        attention_backward_kernel,
        in_specs=[vmem] * 5,
        out_specs=vmem,
        out_shape=jax.ShapeDtypeStruct(qkv.shape, BF),
        compiler_params=pltpu.CompilerParams(vmem_limit_bytes=32 << 20),
        name="attention_backward",
    )(qkv, mixed, grad_mixed, probs_low, probs_high)


def local(
    tokens,
    deal,
    lengths,
    priority,
    routes,
    gain_attn,
    w_query,
    w_key,
    w_value,
    w_out,
    gain_ffn,
    w_router,
    w_gate,
    w_up,
    w_down,
    cotangent,
):
    owners = ("dp", "tensor")
    n_dp = lax.axis_size("dp")
    n_tensor = lax.axis_size("tensor")
    n_expert = lax.axis_size("expert")
    n_owner = n_dp * n_tensor
    local_experts = EXPERTS // n_expert
    outer = n_dp // local_experts
    assert n_tensor == 2 and outer * local_experts == n_dp
    dp_index = lax.axis_index("dp")
    tensor_index = lax.axis_index("tensor")
    expert_index = lax.axis_index("expert")
    inner_index = dp_index % local_experts
    inner_groups = [
        [group * local_experts + at for at in range(local_experts)] for group in range(outer)
    ]
    outer_groups = [
        [group * local_experts + at for group in range(outer)] for at in range(local_experts)
    ]
    rows_own = SEQ_LEN // n_expert
    width = D // n_owner
    chunk = D // n_dp
    head_lanes = HEADS // n_expert * HEAD_DIM
    kv_lanes = KV_HEADS // n_expert * HEAD_DIM
    lower_core = tensor_index == 0

    def across_inner(block):
        if outer == 1:
            return lax.all_to_all(block, "dp", 0, 0, tiled=True)
        return lax.all_to_all(block, "dp", 0, 0, tiled=True, axis_index_groups=inner_groups)

    def gather_dp(block):
        spread = jnp.broadcast_to(block[None], (n_dp,) + block.shape)
        return lax.all_to_all(spread, "dp", 0, 0, tiled=True)

    def both_cores(block, axis):
        other = swap(block, "tensor", 1)
        low = jnp.where(lower_core, block, other)
        high = jnp.where(lower_core, other, block)
        return jnp.stack([low, high], axis=axis)

    routes_t = routes.T.reshape(TOP, MICRO, SEQ_LEN)
    table = jnp.stack(
        [
            priority.reshape(MICRO, SEQ_LEN),
            routes_t[0],
            routes_t[1],
            jnp.broadcast_to(lengths[:, None], (MICRO, SEQ_LEN)),
        ],
        axis=1,
    )
    tables = lax.all_gather(table, owners, axis=0, tiled=True)
    small = jnp.concatenate([w_router.T, gain_attn[None], gain_ffn[None]], axis=0)
    smalls = lax.all_gather(small, owners, axis=0)
    smalls = smalls.transpose(1, 0, 2).reshape(EXPERTS + 2, D)
    router_t = smalls[:EXPERTS]
    gain_one = smalls[EXPERTS].astype(F32)[None]
    gain_two = smalls[EXPERTS + 1].astype(F32)[None]

    w_qkv = gather_dp(jnp.concatenate([w_query, w_key, w_value], axis=1))
    w_qkv = both_cores(w_qkv, 1).reshape(D, head_lanes + 2 * kv_lanes)

    normed_one = []
    qkv_rows = []
    mixed_rows = []
    probs_kept = []
    sequence_tables = []
    for micro in range(MICRO):
        rows = slice(micro * SEQ_LEN, (micro + 1) * SEQ_LEN)
        inputs = tokens[rows].astype(F32)
        normed = (inputs * rms_scale(inputs) * gain_one).astype(BF)
        qkv = matmul(normed, w_qkv).astype(BF)
        own_table = pick(tables, deal[micro])
        mixed, probs_low, probs_high = attention_forward(own_table[3, 0], qkv)
        normed_one.append(normed)
        qkv_rows.append(qkv)
        mixed_rows.append(mixed)
        probs_kept.append((probs_low, probs_high))
        sequence_tables.append(own_table)

    w_out_part = gather_dp(w_out.T)
    w_out_parts = [w_out_part] + [swap(w_out_part, "expert", far) for far in range(1, n_expert)]
    w_out_t = both_cores(jnp.concatenate(w_out_parts, axis=2), 1)
    w_out_t = w_out_t.reshape(D, n_expert * head_lanes)

    def collect(weight):
        if outer > 1:
            weight = lax.all_gather(weight, "dp", axis=0, axis_index_groups=outer_groups)
            weight = across_inner(jnp.swapaxes(weight, 0, 1))
            weight = jnp.swapaxes(weight, 0, 1)
            return weight.reshape((n_dp,) + weight.shape[2:])
        return across_inner(weight)

    def with_other(weight, axis):
        return jnp.concatenate([weight, swap(weight, "tensor", 1)], axis=axis)

    half_ff = w_gate.shape[2]
    gate_weight = with_other(collect(w_gate).reshape(D, half_ff), 1)
    up_weight = with_other(collect(w_up).reshape(D, half_ff), 1)
    down_weight = with_other(collect(w_down).transpose(1, 0, 2).reshape(half_ff, D), 0)

    positions = jnp.arange(SEQ_LEN, dtype=jnp.int32)
    expert_ids = expert_index * local_experts + jnp.bitwise_xor(
        inner_index, jnp.arange(local_experts, dtype=jnp.int32)
    )
    places = jnp.arange(CAP, dtype=F32)[None, :, None]

    def nearest_first(lanes):
        blocks = lanes.reshape(local_experts, n_expert, rows_own)
        return jnp.concatenate(
            [
                lax.dynamic_index_in_dim(blocks, expert_index ^ far, 1, keepdims=False)
                for far in range(n_expert)
            ],
            axis=1,
        )

    def selections(own_table):
        rank, first, second, live_count = own_table
        live = positions < live_count
        wanted = expert_ids[:, None]
        chosen = ((first[None] == wanted) | (second[None] == wanted)) & live[None]
        chosen = chosen.astype(BF)
        earlier = (rank[:, None] < rank[None, :]).astype(BF)
        place = matmul(chosen, earlier)
        place = jnp.where(chosen > 0, place, -1.0)
        given = (place[:, None, :] == places).astype(BF)
        near = (nearest_first(place)[:, None, :] == places).astype(BF)
        return given, near

    def to_experts(given, rows):
        blocks = [matmul(given[far], rows).astype(BF) for far in range(local_experts)]
        return jnp.concatenate(
            [blocks[0]] + [swap(blocks[far], "dp", far) for far in range(1, local_experts)], axis=0
        )

    def from_experts(near, slots):
        blocks = [slots[far * CAP : (far + 1) * CAP] for far in range(local_experts)]
        slots = jnp.concatenate(
            [blocks[0]] + [swap(blocks[far], "dp", far) for far in range(1, local_experts)], axis=0
        )
        near = near.reshape(local_experts * CAP, n_expert, rows_own)
        parts = [matmul_tn(near[:, far], slots).astype(BF) for far in range(n_expert)]
        return sum_over_groups(parts)

    def sum_over_groups(parts):
        total = parts[0].astype(F32)
        for far in range(1, n_expert):
            total = total + swap(parts[far], "expert", far).astype(F32)
        return total

    def own_rows(array, micro):
        start = micro * SEQ_LEN + expert_index * rows_own
        return lax.dynamic_slice_in_dim(array, start, rows_own, 0)

    def spread_rows(blocks):
        whole = jnp.zeros((MICRO * SEQ_LEN, D), BF)
        for micro, block in enumerate(blocks):
            for far in range(n_expert):
                piece = swap(block, "expert", far) if far else block
                start = micro * SEQ_LEN + (expert_index ^ far) * rows_own
                whole = lax.dynamic_update_slice(whole, piece, (start, 0))
        return whole

    chosen_expert = expert_index * local_experts + inner_index
    expert_mask = (jnp.arange(EXPERTS, dtype=jnp.int32) == chosen_expert).astype(F32)[None]

    selected = [selections(sequence_tables[micro]) for micro in range(MICRO)]
    grad_slots = [
        to_experts(selected[micro][0], cotangent[micro * SEQ_LEN : (micro + 1) * SEQ_LEN])
        for micro in range(MICRO)
    ]

    mixed_own = []
    hidden_own = []
    scale_own = []
    slot_rows = []
    for micro in range(MICRO):
        pieces = mixed_rows[micro].reshape(n_expert, rows_own, head_lanes)
        mixed_all = jnp.concatenate(
            [pick(pieces, expert_index)]
            + [
                swap(pick(pieces, expert_index ^ far), "expert", far)
                for far in range(1, n_expert)
            ],
            axis=1,
        )
        hidden_one = own_rows(tokens, micro).astype(F32) + matmul_nt(mixed_all, w_out_t)
        scale_two = rms_scale(hidden_one)
        normed_two = (hidden_one * scale_two * gain_two).astype(BF)
        normed_all = jnp.concatenate(
            [normed_two] + [swap(normed_two, "expert", far) for far in range(1, n_expert)], axis=0
        )
        slot_rows.append(to_experts(selected[micro][1], normed_all))
        mixed_own.append(mixed_all)
        hidden_own.append(hidden_one)
        scale_own.append(scale_two)

    result_own = []
    grad_hidden_own = []
    grad_two_own = []
    hidden_scaled = []
    grads_gate = []
    grads_up = []
    router_grad = 0.0
    for micro in range(MICRO):
        slots = slot_rows[micro]
        cots = grad_slots[micro]
        logits = matmul_nt(slots, router_t)
        router = jax.nn.softmax(logits, axis=-1)
        gates = jnp.sum(router * expert_mask, axis=1, keepdims=True)
        gate_in = matmul(slots, gate_weight)
        up_in = matmul(slots, up_weight)
        cot_hidden = matmul_nt(cots, down_weight)
        sigmoid_in = jax.nn.sigmoid(gate_in)
        activated = gate_in * sigmoid_in
        hidden_float = activated * up_in
        hidden = hidden_float.astype(BF)
        grad_hidden = gates * cot_hidden
        grad_gate_in = (
            grad_hidden * up_in * (sigmoid_in * (1.0 + gate_in * (1.0 - sigmoid_in)))
        ).astype(BF)
        grad_up_in = (grad_hidden * activated).astype(BF)
        gate_grad = jnp.sum(hidden.astype(F32) * cot_hidden, axis=1, keepdims=True)
        grad_logits = (gate_grad * gates * (expert_mask - router)).astype(BF)
        grad_rows = (
            matmul_nt(grad_gate_in, gate_weight)
            + matmul_nt(grad_up_in, up_weight)
            + matmul(grad_logits, router_t)
        ).astype(BF)
        grad_two_own.append(from_experts(selected[micro][1], grad_rows))
        expert_out = (gates * matmul(hidden, down_weight)).astype(BF)
        expert_mix = from_experts(selected[micro][1], expert_out)
        result_own.append((hidden_own[micro] + expert_mix).astype(BF))
        router_grad = router_grad + matmul_tn(grad_logits, slots)
        hidden_scaled.append((gates * hidden_float).astype(BF))
        grads_gate.append(grad_gate_in)
        grads_up.append(grad_up_in)

    def over_micro(lefts, rights):
        return sum(matmul_tn(left, right) for left, right in zip(lefts, rights))

    def halves(blocks, at):
        return [block[:, at * half_ff : (at + 1) * half_ff] for block in blocks]

    def join_cores(own, other):
        return own + swap(other.astype(BF), "tensor", 1).astype(F32)

    def scatter_back(pieces):
        if outer > 1:
            pieces = pieces.reshape((outer, local_experts) + pieces.shape[1:])
            pieces = across_inner(jnp.swapaxes(pieces, 0, 1))
            pieces = jnp.swapaxes(pieces, 0, 1)
            pieces = lax.psum_scatter(
                pieces, "dp", scatter_dimension=0, axis_index_groups=outer_groups
            )
            return pieces.astype(F32)
        return across_inner(pieces).astype(F32)

    d_gate = join_cores(
        over_micro(slot_rows, halves(grads_gate, 0)), over_micro(slot_rows, halves(grads_gate, 1))
    )
    d_gate = scatter_back(d_gate.astype(BF).reshape(n_dp, chunk, half_ff))
    d_up = join_cores(
        over_micro(slot_rows, halves(grads_up, 0)), over_micro(slot_rows, halves(grads_up, 1))
    )
    d_up = scatter_back(d_up.astype(BF).reshape(n_dp, chunk, half_ff))
    d_down = join_cores(
        over_micro(halves(hidden_scaled, 0), grad_slots),
        over_micro(halves(hidden_scaled, 1), grad_slots),
    )
    d_down = d_down.astype(BF).reshape(half_ff, n_dp, chunk).transpose(1, 0, 2)
    d_down = scatter_back(d_down)

    grad_hidden_own = []
    gain_two_grad = 0.0
    branch_own = []
    grad_qkv_rows = []
    grad_one_own = []
    for micro in range(MICRO):
        grad_two = grad_two_own[micro]
        hidden_one = hidden_own[micro]
        scale_two = scale_own[micro]
        gain_two_grad = gain_two_grad + jnp.sum(grad_two * hidden_one * scale_two, axis=0)
        weighted = grad_two * gain_two
        inner = jnp.mean(hidden_one * weighted, axis=-1, keepdims=True)
        grad_hidden_one = (
            own_rows(cotangent, micro).astype(F32)
            + scale_two * weighted
            - hidden_one * (scale_two * scale_two * scale_two) * inner
        )
        grad_branch = grad_hidden_one.astype(BF)
        grad_mixed = matmul(grad_branch, w_out_t).astype(BF)
        pieces = [
            grad_mixed[:, far * head_lanes : (far + 1) * head_lanes] for far in range(n_expert)
        ]
        pieces = [pieces[0]] + [swap(pieces[far], "expert", far) for far in range(1, n_expert)]
        near = jnp.stack(pieces, axis=0)
        grad_heads = jnp.concatenate(
            [pick(near, expert_index ^ at) for at in range(n_expert)], axis=0
        )
        grad_qkv = attention_backward(
            qkv_rows[micro], mixed_rows[micro], grad_heads, *probs_kept[micro]
        )
        blocks = grad_qkv.reshape(n_expert, rows_own, grad_qkv.shape[1])
        parts = [
            matmul_nt(pick(blocks, expert_index ^ far), w_qkv).astype(BF) for far in range(n_expert)
        ]
        grad_one_own.append(sum_over_groups(parts))
        grad_hidden_own.append(grad_hidden_one)
        branch_own.append(grad_branch)
        grad_qkv_rows.append(grad_qkv)

    def split_cores(pieces, axis):
        own = lax.dynamic_index_in_dim(pieces, tensor_index, axis, keepdims=False)
        other = lax.dynamic_index_in_dim(pieces, 1 - tensor_index, axis, keepdims=False)
        return join_cores(own, other)

    def sum_dp(pieces):
        pieces = lax.all_to_all(pieces.astype(BF), "dp", 0, 0, tiled=True)
        return jnp.sum(pieces.astype(F32), axis=0)

    d_out = [
        over_micro(
            branch_own,
            [mixed[:, far * head_lanes : (far + 1) * head_lanes] for mixed in mixed_own],
        )
        .reshape(n_dp, n_tensor, width, head_lanes)
        for far in range(n_expert)
    ]
    d_out = [split_cores(part, 1).astype(BF) for part in d_out]
    d_out = sum_dp(sum_over_groups(d_out)).T

    d_qkv = over_micro(normed_one, grad_qkv_rows)
    d_qkv = split_cores(d_qkv.reshape(n_dp, n_tensor, width, d_qkv.shape[1]), 1)
    d_qkv = sum_dp(d_qkv)

    gain_one_grad = 0.0
    grad_inputs_own = []
    for micro in range(MICRO):
        grad_one = grad_one_own[micro]
        inputs = own_rows(tokens, micro).astype(F32)
        scale_one = rms_scale(inputs)
        gain_one_grad = gain_one_grad + jnp.sum(grad_one * inputs * scale_one, axis=0)
        weighted = grad_one * gain_one
        inner = jnp.mean(inputs * weighted, axis=-1, keepdims=True)
        grad_inputs = (
            grad_hidden_own[micro]
            + scale_one * weighted
            - inputs * (scale_one * scale_one * scale_one) * inner
        )
        grad_inputs_own.append(grad_inputs.astype(BF))

    everywhere = ("dp", "expert", "tensor")
    owner_index = lax.axis_index(owners)
    early = lax.psum(jnp.concatenate([router_grad, gain_two_grad[None]], axis=0), everywhere)
    early = lax.dynamic_slice_in_dim(early, owner_index * width, width, 1)
    late = lax.psum(gain_one_grad, everywhere)
    late = lax.dynamic_slice_in_dim(late, owner_index * width, width, 0)

    return (
        spread_rows(result_own),
        spread_rows(grad_inputs_own),
        late,
        d_qkv[:, :head_lanes],
        d_qkv[:, head_lanes : head_lanes + kv_lanes],
        d_qkv[:, head_lanes + kv_lanes :],
        d_out,
        early[EXPERTS],
        early[:EXPERTS].T,
        d_gate,
        d_up,
        d_down,
    )


def solution(mesh):
    placed = (
        P(("dp", "tensor"), None),
        P(("dp", "tensor")),
        P(("dp", "tensor")),
        P(("dp", "tensor")),
        P(("dp", "tensor"), None),
        P(("dp", "tensor")),
        P(("dp", "tensor"), "expert"),
        P(("dp", "tensor"), "expert"),
        P(("dp", "tensor"), "expert"),
        P("expert", ("dp", "tensor")),
        P(("dp", "tensor")),
        P(("dp", "tensor"), None),
        P("expert", "dp", "tensor"),
        P("expert", "dp", "tensor"),
        P("expert", "tensor", "dp"),
        P(("dp", "tensor"), None),
    )
    return jax.shard_map(
        local,
        mesh=mesh,
        in_specs=placed,
        out_specs=(
            P(("dp", "tensor"), None),
            P(("dp", "tensor"), None),
            P(("dp", "tensor")),
            P(("dp", "tensor"), "expert"),
            P(("dp", "tensor"), "expert"),
            P(("dp", "tensor"), "expert"),
            P("expert", ("dp", "tensor")),
            P(("dp", "tensor")),
            P(("dp", "tensor"), None),
            P("expert", "dp", "tensor"),
            P("expert", "dp", "tensor"),
            P("expert", "tensor", "dp"),
        ),
        check_vma=False,
    )
```
